32 devices in a mesh: dp: 4 (over y, x), seq: 8 (over z, core).
Axes of the slice: x: 2, y: 2, z: 4, core: 2. Of those that a mesh axis runs over, the one named last changes fastest.
Arguments:
- stream: float32 [4, 1024, 2560], P('dp', 'seq'), may hold values from -6 to 6
- seg_ids: int32 [4, 1024], P('dp', 'seq'), may hold values from 0 to 3, never falling along the last dimension, each value on 1 to 512 neighbouring positions
- rec_weight: bfloat16 [2560, 3, 2560], P(('dp', 'seq')), may hold values from -0.125 to 0.125
- gate_weight: bfloat16 [2560, 2, 256], P(('dp', 'seq')), may hold values from -0.375 to 0.375
- mlp_weight: bfloat16 [7680, 3, 2560], P(('dp', 'seq')), may hold values from -0.125 to 0.125
- norm_gains: bfloat16 [2, 2560], P(None, ('dp', 'seq')), may hold values from 0.5 to 1.5
- conv_weight: bfloat16 [4, 2560], P(None, ('dp', 'seq')), may hold values from -3 to 3
- lru_biases: bfloat16 [3, 2560], P(None, ('dp', 'seq')), may hold values from -3 to 3
- decay_param: bfloat16 [2560], P(('dp', 'seq')), may hold values from -15 to -2
- cotangent: float32 [4, 1024, 2560], P('dp', 'seq'), may hold values from -6 to 6
Outputs:
- out_stream: float32 [4, 1024, 2560], P('dp', 'seq')
- stream_grad: float32 [4, 1024, 2560], P('dp', 'seq')
- rec_weight_grad: float32 [2560, 3, 2560], P(('dp', 'seq'))
- gate_weight_grad: float32 [2560, 2, 256], P(('dp', 'seq'))
- mlp_weight_grad: float32 [7680, 3, 2560], P(('dp', 'seq'))
- norm_gains_grad: float32 [2, 2560], P(None, ('dp', 'seq'))
- conv_weight_grad: float32 [4, 2560], P(None, ('dp', 'seq'))
- lru_biases_grad: float32 [3, 2560], P(None, ('dp', 'seq'))
- decay_param_grad: float32 [2560], P(('dp', 'seq'))
The draws below stay inside these ranges and needn't reach their ends.
Inputs may be any that keep to these rules, and one draw needn't show every extreme that they name: `seg_ids`: along each sequence the ids never fall; each id names one document of 1 to 512 tokens, and one document has exactly 512 tokens.
All inputs are finite; a program needn't handle non-finite values.
Results may differ from the reference program's by a relative error of at most 0.014.
Values may be sent and summed in bfloat16 or wider, within the bound.
No kernel may reach another device: no remote copies, remote signals or barrier semaphores. Data moves between devices by JAX's collectives and lax.ppermute only.
A program may use at most 960 MiB of HBM per device.

```python
import math
import jax
import jax.numpy as jnp
import numpy as np
from jax import lax

D = 2560
LRU = 2560
FF = 7680
CONV = 4
HEAD = 256
SEQS = 4
SEQLEN = 1024
DOCS = 4
DOC_MOST = 512


def draw_decay_param(key, part):
    pick_key, slow_key, fast_key = jax.random.split(key, 3)
    slow_share = 0.5
    slow_flag = jax.random.uniform(pick_key, (LRU,), jnp.float32) < slow_share
    slow_rate = jnp.exp(jax.random.uniform(slow_key, (LRU,), jnp.float32, jnp.log(0.05), 0.0)) / (8.0 * DOC_MOST)
    fast_rate = jnp.exp(jax.random.uniform(fast_key, (LRU,), jnp.float32, jnp.log(0.01), jnp.log(0.05)))
    rate_vals = jnp.where(slow_flag, slow_rate, fast_rate)
    return jnp.log(jnp.expm1(rate_vals)).astype(jnp.bfloat16)


def shard_levels(stream_key, shape, cuts, smallest, high):
    loudness = 1.0
    for axis_at, blocks in cuts:
        steps = jax.random.uniform(jax.random.fold_in(jax.random.fold_in(stream_key, 6), axis_at), (blocks,), jnp.float32, smallest / len(cuts), high / len(cuts))
        loudness = loudness * jnp.repeat(jnp.exp(steps), shape[axis_at] // blocks).reshape((-1,) + (1,) * (len(shape) - 1 - axis_at))
    return loudness


def split_up(number_of, total, bound, slope):
    portions = [(1 << 20) // math.isqrt(grade ** slope) + 1 for grade in range(2, number_of + 1)]
    surplus, holding = total - bound - (number_of - 1), [1] * (number_of - 1)
    while surplus > 0:
        free = [i for i in range(number_of - 1) if holding[i] < bound]
        whole, remaining = sum([portions[i] for i in free]), surplus
        for i in free:
            addition = min(bound - holding[i], max(1, remaining * portions[i] // whole), surplus)
            holding[i] = holding[i] + addition
            surplus = surplus - addition
    return np.array([bound] + holding)


def uneven_parts(own_key, count, total, most, skew):
    if count == 2:
        one = jax.random.randint(own_key, (), max(1, total - most), min(most, total - 1) + 1)
        return jnp.stack([one, total - one])
    sizes = jnp.asarray(split_up(count, total, most, skew), jnp.int32)
    twos = (count - 1) // 2
    giver, receiver = sizes[1:1 + 2 * twos:2], sizes[2:2 + 2 * twos:2]
    margin = jnp.minimum(giver - 1, most - receiver)
    passed = jax.random.randint(jax.random.fold_in(own_key, 1), (twos,), 0, 1 << 20) % (margin + 1)
    sizes = sizes.at[1:1 + 2 * twos:2].set(giver - passed).at[2:2 + 2 * twos:2].set(receiver + passed)
    return sizes[jax.random.permutation(jax.random.fold_in(own_key, 2), count)]


def scatter_about(rng, shape, deviation, limit, pieces=(), dtype=jnp.bfloat16):
    result = jax.random.normal(rng, shape, jnp.float32) * deviation
    if len(pieces) > 0:
        result = shard_levels(rng, shape, pieces, -0.22, 0.18) * result
    return jnp.clip(result, min=-limit, max=limit).astype(dtype)


def setup_inputs(seed: int = 0) -> dict:
    keys = jax.random.split(jax.random.key(seed), 11)
    return {
        "stream": scatter_about(keys[0], (SEQS, SEQLEN, D), 1.0, 6.0, ((0, 4), (1, 8)), jnp.float32),
        "seg_ids": jax.vmap(lambda own: jnp.searchsorted(jnp.cumsum(uneven_parts(own, DOCS, SEQLEN, DOC_MOST, 0)), jnp.arange(SEQLEN), side="right"))(jax.random.split(keys[1], SEQS)).reshape((SEQS, SEQLEN)).astype(jnp.int32),
        "rec_weight": scatter_about(keys[2], (LRU, 3, D), D ** -0.5, 0.125, ((0, 32),)),
        "gate_weight": scatter_about(keys[3], (LRU, 2, HEAD), HEAD ** -0.5, 0.375, ((0, 32),)),
        "mlp_weight": scatter_about(keys[4], (FF, 3, D), D ** -0.5, 0.125, ((0, 32),)),
        "norm_gains": jnp.clip(1.0 + 0.1 * jax.random.normal(keys[5], (2, D), jnp.float32), 0.5, 1.5).astype(jnp.bfloat16),
        "conv_weight": scatter_about(keys[6], (CONV, LRU), CONV ** -0.5, 3.0, ((1, 32),)),
        "lru_biases": scatter_about(keys[7], (3, LRU), 0.5, 3.0, ((1, 32),)),
        "decay_param": draw_decay_param(jax.random.fold_in(keys[10], 71), 0),
        "cotangent": scatter_about(keys[9], (SEQS, SEQLEN, D), 1.0, 6.0, ((0, 4), (1, 8)), jnp.float32),
    }


EPS = 1e-06
GELU_ROOT = 0.7978845608028654
GELU_CUBE = 0.044715

def gelu_tanh(values):
    inner_arg = GELU_ROOT * (values + GELU_CUBE * values * values * values)
    return 0.5 * values * (1.0 + jnp.tanh(inner_arg))

def gelu_slope(values):
    inner_arg = GELU_ROOT * (values + GELU_CUBE * values * values * values)
    tanh_value = jnp.tanh(inner_arg)
    return 0.5 * (1.0 + tanh_value) + 0.5 * values * (1.0 - tanh_value * tanh_value) * GELU_ROOT * (1.0 + 3.0 * GELU_CUBE * values * values)

def rms_norm(stream, gain_vec):
    scaling = lax.rsqrt(lax.optimization_barrier(jnp.mean(stream * stream, axis=-1, keepdims=True)) + EPS)
    return stream * scaling * gain_vec

def gate_terms(rate_pre, input_pre, decay_raw, conv_vals, reset_mask):
    recur_gate = jax.nn.sigmoid(rate_pre)
    admit_gate = jax.nn.sigmoid(input_pre)
    log_decay = -8.0 * jax.nn.softplus(decay_raw) * (0.5 + 0.5 * recur_gate)
    decay_factor = jnp.where(reset_mask, 0.0, jnp.exp(log_decay))
    input_scale = jnp.where(reset_mask, 1.0, jnp.sqrt(-jnp.expm1(2.0 * log_decay)))
    return (decay_factor, input_scale * admit_gate * conv_vals)

def affine(earlier_elem, later_elem):
    return (earlier_elem[0] * later_elem[0], later_elem[0] * earlier_elem[1] + later_elem[1])

def conv_apply(ext_values, ext_ids, doc_ids, conv_taps, conv_bias):
    seq_len = doc_ids.shape[0]
    tap_count = conv_taps.shape[0]
    summed = jnp.broadcast_to(conv_bias, (seq_len, conv_bias.shape[0]))
    for lag_index in range(tap_count):
        low_edge = tap_count - 1 - lag_index
        same_doc = (ext_ids[low_edge:low_edge + seq_len] == doc_ids + 1)[:, None]
        summed = summed + jnp.where(same_doc, conv_taps[lag_index] * ext_values[low_edge:low_edge + seq_len], 0.0)
    return summed

def conv_back(ext_grads, ext_next_ids, doc_ids, conv_taps):
    seq_len = doc_ids.shape[0]
    tap_count = conv_taps.shape[0]
    summed = jnp.zeros((seq_len, conv_taps.shape[1]), jnp.float32)
    for lag_index in range(tap_count):
        same_doc = (ext_next_ids[lag_index:lag_index + seq_len] == doc_ids + 1)[:, None]
        summed = summed + jnp.where(same_doc, conv_taps[lag_index] * ext_grads[lag_index:lag_index + seq_len], 0.0)
    return summed

def conv_tap_grad(conv_grad, ext_values, ext_ids, doc_ids, tap_count):
    seq_len = doc_ids.shape[0]
    tap_rows = []
    for lag_index in range(tap_count):
        low_edge = tap_count - 1 - lag_index
        same_doc = (ext_ids[low_edge:low_edge + seq_len] == doc_ids + 1)[:, None]
        tap_rows.append(lax.optimization_barrier(jnp.sum(jnp.where(same_doc, conv_grad * ext_values[low_edge:low_edge + seq_len], 0.0), axis=0)))
    return jnp.stack(tap_rows)

def block_gate(conv16, gate_weight, gate_index):
    seq_len, lru_width = conv16.shape
    head_size = gate_weight.shape[2]
    head_count = lru_width // head_size
    gate_mat = gate_weight[:, gate_index, :].astype(jnp.float32).reshape(head_count, head_size, head_size)
    grouped = conv16.astype(jnp.float32).reshape(seq_len, head_count, head_size)
    return jnp.einsum('thi,hij->thj', grouped, gate_mat).reshape(seq_len, lru_width)

def block_gate_back(grad16, gate_weight, gate_index):
    seq_len, lru_width = grad16.shape
    head_size = gate_weight.shape[2]
    head_count = lru_width // head_size
    gate_mat = gate_weight[:, gate_index, :].astype(jnp.float32).reshape(head_count, head_size, head_size)
    grouped = grad16.astype(jnp.float32).reshape(seq_len, head_count, head_size)
    return jnp.einsum('thj,hij->thi', grouped, gate_mat).reshape(seq_len, lru_width)

def gate_grads(conv16, grad16, head_size):
    seq_len, lru_width = conv16.shape
    head_count = lru_width // head_size
    left_part = conv16.astype(jnp.float32).reshape(seq_len, head_count, head_size)
    right_part = grad16.astype(jnp.float32).reshape(seq_len, head_count, head_size)
    return jnp.einsum('thi,thj->hij', left_part, right_part).reshape(lru_width, head_size)

def one_sequence(resid_in, doc_ids, out_grad, params):
    rec_weight, gate_weight, mlp_weight, norm_gains, conv_weight, lru_biases, decay_param = params
    seq_len = resid_in.shape[0]
    tap_count = conv_weight.shape[0]
    lru_width = rec_weight.shape[0]
    head_size = gate_weight.shape[2]
    gain_one = norm_gains[0].astype(jnp.float32)
    gain_two = norm_gains[1].astype(jnp.float32)
    conv_taps = conv_weight.astype(jnp.float32)
    bias_vals = lru_biases.astype(jnp.float32)
    decay_raw = decay_param.astype(jnp.float32)
    w_in_x = rec_weight[:, 0, :]
    w_in_y = rec_weight[:, 1, :]
    w_out = rec_weight[:, 2, :]
    w_gate = mlp_weight[:, 0, :]
    w_up = mlp_weight[:, 1, :]
    w_down = mlp_weight[:, 2, :]
    normed_in = rms_norm(resid_in, gain_one).astype(jnp.bfloat16)
    x_branch = jnp.dot(normed_in, w_in_x.T, preferred_element_type=jnp.float32).astype(jnp.bfloat16)
    y_pre = jnp.dot(normed_in, w_in_y.T, preferred_element_type=jnp.float32)
    ext_values = jnp.concatenate([jnp.zeros((tap_count - 1, lru_width), jnp.float32), x_branch.astype(jnp.float32)], axis=0)
    ext_ids = jnp.concatenate([jnp.zeros((tap_count - 1,), jnp.int32), (doc_ids + 1).astype(jnp.int32)], axis=0)
    conv_out = conv_apply(ext_values, ext_ids, doc_ids, conv_taps, bias_vals[0]).astype(jnp.bfloat16)
    rate_pre = block_gate(conv_out, gate_weight, 0) + bias_vals[1]
    input_pre = block_gate(conv_out, gate_weight, 1) + bias_vals[2]
    reset_mask = (ext_ids[tap_count - 2:tap_count - 2 + seq_len] != doc_ids + 1)[:, None]
    conv_vals = conv_out.astype(jnp.float32)
    decay_factor, drive = gate_terms(rate_pre, input_pre, decay_raw, conv_vals, reset_mask)
    _, state = lax.associative_scan(affine, (decay_factor, drive), axis=0)
    y_act = gelu_tanh(y_pre)
    mixed_rec = (state * y_act).astype(jnp.bfloat16)
    resid_mid = resid_in + jnp.dot(mixed_rec, w_out, preferred_element_type=jnp.float32)
    normed_mid = rms_norm(resid_mid, gain_two).astype(jnp.bfloat16)
    gate_pre = jnp.dot(normed_mid, w_gate.T, preferred_element_type=jnp.float32)
    up_pre = jnp.dot(normed_mid, w_up.T, preferred_element_type=jnp.float32)
    hidden = (gelu_tanh(gate_pre) * up_pre).astype(jnp.bfloat16)
    out_stream = resid_mid + jnp.dot(hidden, w_down, preferred_element_type=jnp.float32)
    grad_mixed = out_grad.astype(jnp.bfloat16)
    hidden_grad = jnp.dot(grad_mixed, w_down.T, preferred_element_type=jnp.float32)
    gate_grad = (hidden_grad * up_pre * gelu_slope(gate_pre)).astype(jnp.bfloat16)
    up_grad = (hidden_grad * gelu_tanh(gate_pre)).astype(jnp.bfloat16)
    mlp_grad = jnp.stack([jnp.dot(gate_grad.T, normed_mid, preferred_element_type=jnp.float32), jnp.dot(up_grad.T, normed_mid, preferred_element_type=jnp.float32), jnp.dot(hidden.T, grad_mixed, preferred_element_type=jnp.float32)], axis=1)
    normed_mid_grad = jnp.dot(gate_grad, w_gate, preferred_element_type=jnp.float32) + jnp.dot(up_grad, w_up, preferred_element_type=jnp.float32)
    _, norm_pull = jax.vjp(rms_norm, resid_mid, gain_two)
    resid_norm_grad, gain_two_grad = norm_pull(normed_mid_grad)
    resid_grad = out_grad + resid_norm_grad
    resid_grad_b = resid_grad.astype(jnp.bfloat16)
    mixed_grad = jnp.dot(resid_grad_b, w_out.T, preferred_element_type=jnp.float32)
    state_grad = mixed_grad * y_act
    y_pre_grad = (mixed_grad * state * gelu_slope(y_pre)).astype(jnp.bfloat16)
    decay_next = jnp.concatenate([decay_factor[1:], jnp.zeros((1, lru_width), jnp.float32)], axis=0)
    _, adjoint = lax.associative_scan(affine, (decay_next, state_grad), reverse=True, axis=0)
    state_prev = jnp.concatenate([jnp.zeros((1, lru_width), jnp.float32), state[:-1]], axis=0)

    def gate_map(rate_arg, input_arg, decay_arg, conv_arg):
        return gate_terms(rate_arg, input_arg, decay_arg, conv_arg, reset_mask)
    _, gate_pull = jax.vjp(gate_map, rate_pre, input_pre, decay_raw, conv_vals)
    rate_grad, input_grad, decay_grad, conv_direct = gate_pull((adjoint * state_prev, adjoint))
    rate_grad_b = rate_grad.astype(jnp.bfloat16)
    input_grad_b = input_grad.astype(jnp.bfloat16)
    gate_grad_all = jnp.stack([gate_grads(conv_out, rate_grad_b, head_size), gate_grads(conv_out, input_grad_b, head_size)], axis=1)
    conv_grad = conv_direct + block_gate_back(rate_grad_b, gate_weight, 0) + block_gate_back(input_grad_b, gate_weight, 1)
    tap_grad = conv_tap_grad(conv_grad, ext_values, ext_ids, doc_ids, tap_count)
    bias_grad = jnp.stack([lax.optimization_barrier(jnp.sum(conv_grad, axis=0)), lax.optimization_barrier(jnp.sum(rate_grad, axis=0)), lax.optimization_barrier(jnp.sum(input_grad, axis=0))])
    ext_grads = jnp.concatenate([conv_grad, jnp.zeros((tap_count - 1, lru_width), jnp.float32)], axis=0)
    ext_next_ids = jnp.concatenate([(doc_ids + 1).astype(jnp.int32), jnp.zeros((tap_count - 1,), jnp.int32)], axis=0)
    x_grad = conv_back(ext_grads, ext_next_ids, doc_ids, conv_taps).astype(jnp.bfloat16)
    rec_grad = jnp.stack([jnp.dot(x_grad.T, normed_in, preferred_element_type=jnp.float32), jnp.dot(y_pre_grad.T, normed_in, preferred_element_type=jnp.float32), jnp.dot(mixed_rec.T, resid_grad_b, preferred_element_type=jnp.float32)], axis=1)
    normed_in_grad = jnp.dot(x_grad, w_in_x, preferred_element_type=jnp.float32) + jnp.dot(y_pre_grad, w_in_y, preferred_element_type=jnp.float32)
    _, first_pull = jax.vjp(rms_norm, resid_in, gain_one)
    stream_norm_grad, gain_one_grad = first_pull(normed_in_grad)
    stream_grad = resid_grad + stream_norm_grad
    gains_grad = jnp.stack([gain_one_grad, gain_two_grad])
    return (out_stream, stream_grad, (rec_grad, gate_grad_all, mlp_grad, gains_grad, tap_grad, bias_grad, decay_grad))

def reference(stream, seg_ids, rec_weight, gate_weight, mlp_weight, norm_gains, conv_weight, lru_biases, decay_param, cotangent):
    params = (rec_weight, gate_weight, mlp_weight, norm_gains, conv_weight, lru_biases, decay_param)
    zero_grads = tuple((jnp.zeros(param_arr.shape, jnp.float32) for param_arr in params))

    def step_fn(grads_sum, inputs):
        stream_seq, ids_seq, cot_seq = inputs
        out_seq, grad_seq, grads_seq = one_sequence(stream_seq, ids_seq, cot_seq, params)
        summed = tuple((running + fresh for running, fresh in zip(grads_sum, grads_seq)))
        return (summed, (out_seq, grad_seq))
    grads_sum, outputs = lax.scan(step_fn, zero_grads, (stream, seg_ids, cotangent))
    return (outputs[0], outputs[1], grads_sum[0], grads_sum[1], grads_sum[2], grads_sum[3], grads_sum[4], grads_sum[5], grads_sum[6])
```

```python
import functools

import jax
import jax.numpy as jnp
from jax import lax
from jax.experimental import pallas as pl
from jax.experimental.pallas import tpu as pltpu
from jax.sharding import PartitionSpec as P

EPS = 1e-06
GELU_ROOT = 0.7978845608028654
GELU_CUBE = 0.044715
F32 = jnp.float32
BF16 = jnp.bfloat16


def gelu_tanh(values):
    inner_arg = GELU_ROOT * (values + GELU_CUBE * values * values * values)
    return 0.5 * values * (1.0 + jnp.tanh(inner_arg))


def gelu_both(values):
    inner_arg = GELU_ROOT * (values + GELU_CUBE * values * values * values)
    tanh_value = jnp.tanh(inner_arg)
    half_sum = 0.5 * (1.0 + tanh_value)
    slope = half_sum + 0.5 * values * (1.0 - tanh_value * tanh_value) * GELU_ROOT * (
        1.0 + 3.0 * GELU_CUBE * values * values
    )
    return values * half_sum, slope


def rms_norm(stream, gain_vec):
    scaling = lax.rsqrt(jnp.mean(stream * stream, axis=-1, keepdims=True) + EPS)
    return stream * scaling * gain_vec


def dot(left, right, left_dim, right_dim):
    return lax.dot_general(
        left, right, (((left_dim,), (right_dim,)), ((), ())), preferred_element_type=F32
    )


def join_kernel(*refs):
    pieces, out_ref, sems = refs[:-2], refs[-2], refs[-1]
    copies, start = [], 0
    for n, piece in enumerate(pieces):
        rows = piece.shape[0]
        copies.append(pltpu.make_async_copy(piece, out_ref.at[pl.ds(start, rows)], sems.at[n]))
        start += rows
    for copy in copies:
        copy.start()
    for copy in copies:
        copy.wait()


def join(pieces):
    rows, width = sum(a.shape[0] for a in pieces), pieces[0].shape[1]
    size = rows * width * 2
    return pl.pallas_call(
        join_kernel,
        in_specs=[pl.BlockSpec(memory_space=pl.ANY)] * len(pieces),
        out_specs=pl.BlockSpec(memory_space=pltpu.VMEM),
        out_shape=jax.ShapeDtypeStruct((rows, width), pieces[0].dtype),
        scratch_shapes=[pltpu.SemaphoreType.DMA((len(pieces),))],
        compiler_params=pltpu.CompilerParams(vmem_limit_bytes=56 << 20),
        cost_estimate=pl.CostEstimate(flops=0, bytes_accessed=2 * size, transcendentals=0),
    )(*pieces)


def after(value, *others):
    return lax.optimization_barrier((value,) + others)[0]


def swap(value):
    count = lax.axis_size("seq")
    return lax.ppermute(value, "seq", [(i, i ^ 1) for i in range(count)])


def shift(value, step):
    count = lax.axis_size("seq")
    return lax.ppermute(value, "seq", [(i, (i + 2 * step) % count) for i in range(count)])


def cross(value, bit):
    count = lax.axis_size("dp")
    return lax.ppermute(value, "dp", [(i, i ^ bit) for i in range(count)])


def rows_at(value, chip, offset, size, own):
    chips = lax.axis_size("seq") // 2
    return lax.dynamic_slice(value, ((chip % chips) * own + offset, 0), (size, value.shape[1]))


def gather_chips(own):
    chips, chip = lax.axis_size("seq") // 2, lax.axis_index("seq") // 2
    rows = own.shape[0]
    half = rows // 2
    up, down = own[:half], own[half:]
    whole = jnp.zeros((chips * rows, own.shape[1]), own.dtype)
    whole = lax.dynamic_update_slice(whole, own, (chip * rows, 0))
    for k in range(1, chips):
        up, down = shift(up, 1), shift(down, -1)
        whole = lax.dynamic_update_slice(whole, up, (((chip - k) % chips) * rows, 0))
        whole = lax.dynamic_update_slice(whole, down, (((chip + k) % chips) * rows + half, 0))
    return whole


def scatter_chips(terms):
    chips, chip = lax.axis_size("seq") // 2, lax.axis_index("seq") // 2
    own = terms.shape[0] // chips
    half = own // 2

    def level(k):
        up, down = rows_at(terms, chip - k, 0, half, own), rows_at(terms, chip + k, half, half, own)
        return up.astype(F32), down.astype(F32)

    up, down = level(1 % chips)
    for j in range(1, chips):
        next_up, next_down = level((j + 1) % chips)
        up = next_up + shift(up.astype(BF16), 1).astype(F32)
        down = next_down + shift(down.astype(BF16), -1).astype(F32)
    return jnp.concatenate([up, down], axis=0)


def gather_line(own):
    half = own.shape[0] // 2
    up, down = own[:half], own[half:]
    steps = [[own, swap(own)]]
    for _ in range(1, lax.axis_size("seq") // 2):
        up, down = shift(up, 1), shift(down, -1)
        steps.append([up, down, swap(up), swap(down)])
    return steps


def scatter_line(terms):
    chips = lax.axis_size("seq") // 2

    def level(k):
        keep = terms[k].shape[0] // 2
        mine = terms[k][:keep] + swap(terms[k][keep:].astype(BF16)).astype(F32)
        return mine[: keep // 2], mine[keep // 2 :]

    up, down = level(1 % chips)
    for j in range(1, chips):
        next_up, next_down = level((j + 1) % chips)
        up = next_up + shift(up.astype(BF16), 1).astype(F32)
        down = next_down + shift(down.astype(BF16), -1).astype(F32)
    return jnp.concatenate([up, down], axis=0)


def gather_plane(own):
    half = own.shape[0] // 2
    first, second = cross(own, 1), cross(own, 2)
    third = [cross(first[:half], 2), cross(second[half:], 1)]
    near = [own, first, second] + third
    return join(near + [swap(a) for a in near])


def scatter_plane(mine, other):
    block = mine.shape[0] // 4
    half = block // 2
    far = mine[3 * block :] + swap(other[3 * block :]).astype(F32)
    far = far.astype(BF16)
    near = mine[: 3 * block] + swap(other[: 3 * block]).astype(F32)
    here, first, second = near[:block], near[block : 2 * block], near[2 * block :]
    top, low = cross(far[:half], 2).astype(F32), cross(far[half:], 1).astype(F32)
    first = jnp.concatenate([first[:half] + top, first[half:]], axis=0).astype(BF16)
    second = jnp.concatenate([second[:half], second[half:] + low], axis=0).astype(BF16)
    return here + cross(first, 1).astype(F32) + cross(second, 2).astype(F32)


def gather_pair(own):
    first = cross(own, 1)
    return join([own, swap(own), first, swap(first)])


def small_gather(value):
    dp_count, seq_count = lax.axis_size("dp"), lax.axis_size("seq")
    dp_place, seq_place = lax.axis_index("dp"), lax.axis_index("seq")
    near = jnp.stack([value] + [cross(value, e) for e in range(1, dp_count)])
    rounds = [(lambda i, k=k: (i + k) % seq_count) for k in range(seq_count)]
    every = [near] + [
        lax.ppermute(near, "seq", [(i, to(i)) for i in range(seq_count)]) for to in rounds[1:]
    ]
    every = jnp.stack(every).reshape(seq_count * dp_count, -1)
    spot = jnp.arange(seq_count * dp_count)
    source = ((seq_place - spot // dp_count) % seq_count) * dp_count + ((spot % dp_count) ^ dp_place)
    return dot((source[:, None] == spot[None, :]).astype(BF16), every, 1, 0).astype(BF16)


def small_sum_seq(terms):
    count = lax.axis_size("seq")
    place = lax.axis_index("seq")
    total = lax.dynamic_index_in_dim(terms, place, 0, False)
    for k in range(1, count):
        sent = lax.dynamic_index_in_dim(terms, (place + k) % count, 0, False)
        total = total + lax.ppermute(sent, "seq", [(i, (i + k) % count) for i in range(count)])
    return total


def small_sum_dp(terms):
    count = lax.axis_size("dp")
    place = lax.axis_index("dp")
    total = lax.dynamic_index_in_dim(terms, place, 0, False)
    for k in range(1, count):
        sent = lax.dynamic_index_in_dim(terms, (place + k) % count, 0, False)
        total = total + lax.ppermute(sent, "dp", [(i, (i + k) % count) for i in range(count)])
    return total


def rows_of(index, size):
    return pl.ds(pl.multiple_of(index * size, size), size)


def conv_kernel(parts, order, x_ref, halo_ref, mask_ref, prm_ref, out_ref, buf):
    rows = buf.shape[0] - 8

    def one(i, carry):
        @pl.when(i % parts == 0)
        def _():
            buf[0:8, :] = halo_ref[rows_of(i // parts, 8), :]

        x = x_ref[rows_of(order[i], rows), :].astype(F32)
        buf[8 : 8 + rows, :] = x
        mask = mask_ref[rows_of(i, rows), :]
        total = prm_ref[4:5, :] + jnp.where(mask[:, 0:1] > 0.0, prm_ref[0:1, :] * x, 0.0)
        for k in range(1, 4):
            late = buf[8 - k : 8 - k + rows, :]
            total = total + jnp.where(mask[:, k : k + 1] > 0.0, prm_ref[k : k + 1, :] * late, 0.0)
        out_ref[rows_of(i, rows), :] = total.astype(BF16)
        buf[0:8, :] = x[rows - 8 :, :]
        return carry

    lax.fori_loop(0, x_ref.shape[0] // rows, one, 0)


def minus_expm1(v):
    series = v * (1.0 / 10.0)
    for n in range(9, 1, -1):
        series = (1.0 + series) * v * (1.0 / n)
    return jnp.where(v > -0.5, -v * (1.0 + series), 1.0 - jnp.exp(v))


def gates(rate, admit, prm_ref, start):
    recur_gate = jax.nn.sigmoid(rate + prm_ref[5:6, :])
    admit_gate = jax.nn.sigmoid(admit + prm_ref[6:7, :])
    log_decay = -8.0 * prm_ref[8:9, :] * (0.5 + 0.5 * recur_gate)
    decay = jnp.where(start, 0.0, jnp.exp(log_decay))
    scale = jnp.where(start, 1.0, jnp.sqrt(minus_expm1(2.0 * log_decay)))
    return recur_gate, admit_gate, decay, scale


def scan_rows(mult, add, carry, reverse):
    rows = mult.shape[0]
    place = lax.broadcasted_iota(jnp.int32, mult.shape, 0) % 8
    for step in (1, 2, 4):
        turn = rows - step if reverse else step
        inside = (place < 8 - step) if reverse else (place >= step)
        prev_mult = jnp.where(inside, pltpu.roll(mult, turn, 0), 1.0)
        prev_add = jnp.where(inside, pltpu.roll(add, turn, 0), 0.0)
        add = mult * prev_add + add
        mult = mult * prev_mult
    sums, products = [], []
    order = range(rows // 8)
    for tile in reversed(order) if reverse else order:
        lead = mult[tile * 8 : tile * 8 + 8]
        part = add[tile * 8 : tile * 8 + 8] + lead * carry[0]
        lead = lead * carry[1]
        carry = (part[0:1], lead[0:1]) if reverse else (part[7:8], lead[7:8])
        sums.append(part)
        products.append(lead)
    if reverse:
        sums, products = sums[::-1], products[::-1]
    return jnp.concatenate(sums, axis=0), jnp.concatenate(products, axis=0), carry


def fresh(begin, carry):
    return jnp.where(begin, 0.0, carry[0]), jnp.where(begin, 1.0, carry[1])


def blank(width):
    return jnp.zeros((1, width), F32), jnp.ones((1, width), F32)


def local_kernel(rows, parts, rate_ref, admit_ref, conv_ref, mask_ref, prm_ref, local_ref, lead_ref, decay_ref, recur_ref, enter_ref, scale_ref, ends_ref):
    count = rate_ref.shape[0] // rows

    def one(i, carry):
        here = rows_of(i, rows)
        start = mask_ref[here, :][:, 1:2] < 0.5
        recur_gate, admit_gate, decay, scale = gates(rate_ref[here, :], admit_ref[here, :], prm_ref, start)
        recur_ref[here, :] = recur_gate
        enter_ref[here, :] = admit_gate
        scale_ref[here, :] = scale
        drive = scale * admit_gate * conv_ref[here, :].astype(F32)
        local, lead, carry = scan_rows(decay, drive, fresh(i % parts == 0, carry), False)
        local_ref[here, :] = local
        lead_ref[here, :] = lead
        decay_ref[here, :] = decay
        ends_ref[pl.ds(i // parts, 1), :] = carry[0]
        ends_ref[pl.ds(count // parts + i // parts, 1), :] = carry[1]
        return carry

    lax.fori_loop(0, count, one, blank(rate_ref.shape[1]))


def state_kernel(rows, parts, order, local_ref, lead_ref, y_ref, enter_ref, state_ref, prev_ref, mixed_ref):
    def one(i, carry):
        here, there = rows_of(i, rows), rows_of(order[i], rows)
        enter = enter_ref[pl.ds(i // parts, 1), :]
        carry = jnp.where(i % parts == 0, enter, carry)
        state = local_ref[here, :] + lead_ref[here, :] * enter
        top = lax.broadcasted_iota(jnp.int32, state.shape, 0) == 0
        state_ref[here, :] = state
        prev_ref[here, :] = jnp.where(top, carry, pltpu.roll(state, 1, 0))
        mixed_ref[there, :] = (state * gelu_tanh(y_ref[there, :])).astype(BF16)
        return state[rows - 1 :, :]

    lax.fori_loop(0, local_ref.shape[0] // rows, one, jnp.zeros((1, local_ref.shape[1]), F32))


def flow_kernel(rows, parts, order, grad_ref, y_ref, decay_ref, flow_ref, lead_ref, state_grad_ref, ends_ref):
    count = grad_ref.shape[0] // rows

    def one(lap, carry):
        i = count - 1 - lap
        here, there = rows_of(i, rows), rows_of(order[i], rows)
        state_grad = grad_ref[there, :] * gelu_tanh(y_ref[there, :])
        decay = decay_ref[here, :]
        carry = fresh(i % parts == parts - 1, carry)
        flow, lead, carry = scan_rows(decay, decay * state_grad, carry, True)
        flow_ref[here, :] = flow
        lead_ref[here, :] = lead
        state_grad_ref[here, :] = state_grad
        ends_ref[pl.ds(i // parts, 1), :] = carry[0]
        ends_ref[pl.ds(count // parts + i // parts, 1), :] = carry[1]
        return carry

    lax.fori_loop(0, count, one, blank(grad_ref.shape[1]))


def adjoint_kernel(
    rows, parts, order, flow_ref, lead_ref, state_grad_ref, enter_ref, grad_ref, y_ref, state_ref, prev_ref,
    decay_ref, recur_ref, admit_ref, scale_ref, conv_ref, mask_ref, prm_ref, y_grad_ref, rate_grad_ref, admit_grad_ref, direct_ref, sums_ref,
):
    count = decay_ref.shape[0] // rows
    sums_ref[...] = jnp.zeros_like(sums_ref)

    def one(lap, carry):
        i = count - 1 - lap
        here, there = rows_of(i, rows), rows_of(order[i], rows)
        start = mask_ref[here, :][:, 1:2] < 0.5
        recur_gate, admit_gate = recur_ref[here, :], admit_ref[here, :]
        decay, scale = decay_ref[here, :], scale_ref[here, :]
        conv = conv_ref[here, :].astype(F32)
        _, y_slope = gelu_both(y_ref[there, :])
        y_grad_ref[there, :] = (grad_ref[there, :] * state_ref[here, :] * y_slope).astype(BF16)
        enter = enter_ref[pl.ds(i // parts, 1), :]
        carry = jnp.where(i % parts == parts - 1, enter, carry)
        flow = flow_ref[here, :] + lead_ref[here, :] * enter
        last = lax.broadcasted_iota(jnp.int32, flow.shape, 0) == rows - 1
        adjoint = state_grad_ref[here, :] + jnp.where(last, carry, pltpu.roll(flow, rows - 1, 0))
        scaled = adjoint * scale
        scale_grad = adjoint * admit_gate * conv
        log_grad = jnp.where(
            start, 0.0, adjoint * prev_ref[here, :] * decay - scale_grad * (decay * decay) / scale
        )
        rate_grad = log_grad * (-4.0 * prm_ref[8:9, :]) * (recur_gate * (1.0 - recur_gate))
        admit_grad = scaled * conv * (admit_gate * (1.0 - admit_gate))
        direct_ref[here, :] = scaled * admit_gate
        rate_grad_ref[here, :] = rate_grad.astype(BF16)
        admit_grad_ref[here, :] = admit_grad.astype(BF16)
        sums_ref[0:1, :] += jnp.sum(rate_grad, axis=0, keepdims=True)
        sums_ref[1:2, :] += jnp.sum(admit_grad, axis=0, keepdims=True)
        sums_ref[2:3, :] += jnp.sum(log_grad * (-4.0 - 4.0 * recur_gate), axis=0, keepdims=True)
        return flow[0:1, :]

    lax.fori_loop(0, count, one, jnp.zeros((1, decay_ref.shape[1]), F32))
    sums_ref[2:3, :] = sums_ref[2:3, :] * prm_ref[9:10, :]


def conv_back_kernel(parts, order, grad_ref, x_ref, halo_ref, mask_ref, prm_ref, x_grad_ref, sums_ref, buf):
    rows = buf.shape[0] - 8
    count = grad_ref.shape[0] // rows
    sums_ref[...] = jnp.zeros_like(sums_ref)

    def one(lap, carry):
        i = count - 1 - lap
        here, there = rows_of(i, rows), rows_of(order[i], rows)

        @pl.when(i % parts == parts - 1)
        def _():
            buf[rows : rows + 8, :] = halo_ref[rows_of(i // parts, 8), :]

        grad = grad_ref[here, :]
        buf[0:rows, :] = grad
        x = x_ref[there, :].astype(F32)
        mask = mask_ref[here, :]
        total = jnp.zeros_like(grad)
        for k in range(4):
            late = jnp.where(mask[:, 4 + k : 5 + k] > 0.0, buf[k : k + rows, :], 0.0)
            total = total + prm_ref[k : k + 1, :] * late
            sums_ref[k : k + 1, :] += jnp.sum(late * x, axis=0, keepdims=True)
        sums_ref[4:5, :] += jnp.sum(grad, axis=0, keepdims=True)
        x_grad_ref[there, :] = total.astype(BF16)
        buf[rows : rows + 8, :] = grad[0:8, :]
        return carry

    lax.fori_loop(0, count, one, 0)


def run(kernel, order, inputs, outs, scratch=()):
    whole = pl.BlockSpec(memory_space=pltpu.VMEM)
    table = () if order is None else (order,)
    size = sum(a.size * 4 for a in inputs) + sum(4 * s.size for s in outs)
    return pl.pallas_call(
        kernel,
        in_specs=[pl.BlockSpec(memory_space=pltpu.SMEM)] * len(table) + [whole] * len(inputs),
        out_specs=[whole] * len(outs),
        out_shape=list(outs),
        scratch_shapes=list(scratch),
        compiler_params=pltpu.CompilerParams(vmem_limit_bytes=56 << 20),
        cost_estimate=pl.CostEstimate(flops=50 * size, bytes_accessed=size, transcendentals=size),
    )(*table, *inputs)


def enter_from(ends, reverse):
    chips = lax.axis_size("seq") // 2
    chip = lax.axis_index("seq") // 2
    count = ends.shape[0] // 2
    state = jnp.zeros((count, ends.shape[1]), F32)
    for k in range(chips - 1, 0, -1):
        sent = shift(ends, -k if reverse else k)
        there = (chip + k < chips) if reverse else (chip >= k)
        state = jnp.where(there, sent[:count] + sent[count:] * state, state)
    return state


def per_device(
    stream, seg_ids, rec_weight, gate_weight, mlp_weight, norm_gains, conv_weight, lru_biases, decay_param, cotangent
):
    resid_in, doc_ids, out_grad = stream[0], seg_ids[0], cotangent[0]
    block, width = resid_in.shape
    dp_count, seq_count = lax.axis_size("dp"), lax.axis_size("seq")
    dp_place, seq_place = lax.axis_index("dp"), lax.axis_index("seq")
    chip_place, core_place = seq_place // 2, seq_place % 2
    chips = seq_count // 2
    half = block // 2
    stretch = 2 * block
    tokens = dp_count * stretch
    parts = stretch // half
    shard, head = rec_weight.shape[0], gate_weight.shape[2]
    units = shard * chips
    ff_shard = mlp_weight.shape[0]

    place = jnp.arange(dp_count * parts)
    order = (
        (((place // 2) % 2) ^ core_place) * dp_count + ((place // parts) ^ dp_place)
    ) * 2 + place % 2
    order = order.astype(jnp.int32)

    def unit_id(dp_index, core_index, row):
        return (dp_index * seq_count + (row // shard) * 2 + core_index) * shard + row % shard

    own_unit = unit_id(dp_place, core_place, jnp.arange(units))
    spot = jnp.arange(4 * units)
    pair_unit = unit_id(dp_place ^ (spot // (2 * units)), core_place ^ ((spot // units) % 2), spot % units)
    spot = jnp.arange(8 * units)
    grad_unit = unit_id(
        dp_place ^ (spot // (4 * units)), core_place ^ ((spot // (2 * units)) % 2), spot % units
    )
    grad_kind = (spot // units) % 2

    small = jnp.concatenate([norm_gains, conv_weight, lru_biases, decay_param[None]], axis=0)
    small = jnp.concatenate([small.reshape(-1), doc_ids.astype(BF16)])
    length = small.shape[0]
    small = jnp.pad(small, (0, -length % 128)).reshape(-1, 128)
    small = small_gather(small).reshape(seq_count, dp_count, -1)
    ids = jnp.transpose(small[:, :, 10 * shard : length], (1, 0, 2)).reshape(dp_count, -1).astype(jnp.int32)
    small = small[:, :, : 10 * shard].reshape(seq_count, dp_count, 10, shard)
    small = jnp.transpose(small, (2, 1, 0, 3)).reshape(10, width)
    gain_one, gain_two = small[0].astype(F32), small[1].astype(F32)

    w_x = gather_chips(rec_weight[:, 0, :])
    later = jnp.concatenate(
        [rec_weight[:, 1:, :].reshape(shard, 2 * width), gate_weight.reshape(shard, 2 * head)], axis=1
    )
    later = gather_chips(lax.optimization_barrier((later, w_x))[0])
    w_y, w_o, gate_own = later[:, :width], later[:, width : 2 * width], later[:, 2 * width :]

    own = (jnp.arange(width)[:, None] == own_unit[None, :]).astype(BF16)
    own = dot(small[2:], own, 1, 0)
    decay_raw = own[7]
    params = jnp.concatenate(
        [own, jax.nn.softplus(decay_raw)[None], jax.nn.sigmoid(decay_raw)[None], jnp.zeros((6, units), F32)]
    )
    near_ids = lax.dynamic_slice(
        jnp.pad(ids, ((0, 0), (3, 3)), constant_values=-1), (0, chip_place * stretch), (dp_count, stretch + 6)
    )
    masks = [near_ids[:, 3 : 3 + stretch] == near_ids[:, 3 - k : 3 - k + stretch] for k in range(4)]
    masks += [near_ids[:, 3 : 3 + stretch] == near_ids[:, 3 + k : 3 + k + stretch] for k in range(4)]
    masks = jnp.stack(masks, axis=-1).astype(F32).reshape(tokens, 8)

    normed_in = rms_norm(resid_in, gain_one).astype(BF16)
    all_in = gather_plane(normed_in)
    mlp_rows = after(tuple(mlp_weight[:, n, :] for n in range(3)), all_in)
    w_g, w_u, w_d = (lax.all_gather(a, "dp", axis=0, tiled=True) for a in mlp_rows)
    x_rel = dot(all_in, w_x, 1, 1).astype(BF16)
    shape = lambda dtype: jax.ShapeDtypeStruct((tokens, units), dtype)
    sums = jax.ShapeDtypeStruct((8, units), F32)
    ends = jax.ShapeDtypeStruct((2 * dp_count, units), F32)
    buffer = (pltpu.VMEM((half + 8, units), F32),)
    call = lambda kernel: functools.partial(kernel, half, parts)
    tails = x_rel.reshape(-1, half, units)[:, half - 8 :]
    tails = jnp.take(tails, order[parts - 1 :: parts], axis=0)
    halo = shift(tails, 1).astype(F32).reshape(-1, units)
    (conv_out,) = run(
        functools.partial(conv_kernel, parts), order, (x_rel, halo, masks, params), (shape(BF16),), buffer
    )
    conv_rows = conv_out.T

    gate_pair = gather_pair(gate_own)
    own_column = jnp.concatenate([own_unit % head, own_unit % head + head])
    pick = (jnp.arange(2 * head)[:, None] == own_column[None, :]).astype(BF16)
    own_heads = jnp.concatenate([own_unit // head] * 2)
    spread = jnp.where(
        pair_unit[:, None] // head == own_heads[None, :], dot(gate_pair, pick, 1, 0), 0.0
    ).astype(BF16)
    y_rel = dot(all_in, w_y, 1, 1)
    conv_pair = after(gather_pair(conv_rows), y_rel)
    rate_pre = dot(conv_pair, spread[:, :units], 0, 0)
    admit_pre = dot(conv_pair, spread[:, units:], 0, 0)
    local, lead, decay, recur_gate, admit_gate, scale, tops = run(
        call(local_kernel), None, (rate_pre, admit_pre, conv_out, masks, params), (shape(F32),) * 6 + (ends,)
    )
    state, state_prev, mixed = run(
        call(state_kernel), order, (local, lead, y_rel, enter_from(tops, False)),
        (shape(F32), shape(F32), shape(BF16)),
    )
    mid = tokens // 2
    resid_mid = resid_in + scatter_plane(
        dot(mixed[:mid], w_o, 1, 0), dot(mixed[mid:], w_o, 1, 0).astype(BF16)
    )

    normed_mid = rms_norm(resid_mid, gain_two).astype(BF16)
    grad_steps = gather_line(lax.optimization_barrier((out_grad.astype(BF16), w_o))[0])
    mid_steps = gather_line(normed_mid)
    group = max(1, chips // 2)
    hidden, gate_grad, up_grad, mids, grads = [], [], [], [], []
    for k in range(0, chips, group):
        mid_rows = join([a for step in mid_steps[k : k + group] for a in step])
        grad_rows = join([a for step in grad_steps[k : k + group] for a in step])
        gate_pre, up_pre = dot(mid_rows, w_g, 1, 1), dot(mid_rows, w_u, 1, 1)
        hidden_grad = dot(grad_rows, w_d, 1, 1)
        act, slope = gelu_both(gate_pre)
        hidden.append((act * up_pre).astype(BF16))
        gate_grad.append((hidden_grad * up_pre * slope).astype(BF16))
        up_grad.append((hidden_grad * act).astype(BF16))
        mids.append(mid_rows)
        grads.append(grad_rows)

    def step(groups, k):
        return groups[k // group][(k % group) * stretch : (k % group + 1) * stretch]

    mid_terms = [
        dot(step(gate_grad, k), w_g, 1, 0) + dot(step(up_grad, k), w_u, 1, 0) for k in range(chips)
    ]
    mid_grad = scatter_line(mid_terms)
    cols = after((join(gate_grad), join(up_grad), join(hidden), join(mids), join(grads)), *mid_terms)
    sums_g = dot(cols[0], cols[3], 0, 0).astype(BF16)
    sums_u = dot(cols[1], cols[3], 0, 0).astype(BF16)
    sums_d = dot(cols[2], cols[4], 0, 0).astype(BF16)
    mid_grad = after(mid_grad, sums_g, sums_u, sums_d)
    mlp_grad = jnp.stack(
        [lax.psum_scatter(a, "dp", scatter_dimension=0, tiled=True) for a in (sums_g, sums_u, sums_d)], axis=1
    ).astype(F32)

    _, norm_pull = jax.vjp(rms_norm, resid_mid, gain_two)
    resid_norm_grad, gain_two_grad = norm_pull(mid_grad)
    resid_grad = out_grad + resid_norm_grad
    all_resid = gather_plane(resid_grad.astype(BF16))
    mixed_grad = dot(all_resid, w_o, 1, 1)
    flow, flow_lead, state_grad, heads_up = run(
        call(flow_kernel), order, (mixed_grad, y_rel, decay), (shape(F32), shape(F32), shape(F32), ends)
    )
    y_grad, rate_grad, admit_grad, direct, gate_sums = run(
        call(adjoint_kernel), order,
        (
            flow, flow_lead, state_grad, enter_from(heads_up, True), mixed_grad, y_rel, state, state_prev,
            decay, recur_gate, admit_gate, scale, conv_out, masks, params,
        ),
        (shape(BF16), shape(BF16), shape(BF16), shape(F32), sums),
    )
    grad_pair = gather_pair(jnp.concatenate([rate_grad.T, admit_grad.T], axis=0))
    chosen = (
        jnp.arange(2 * head)[:, None] == (grad_unit % head + grad_kind * head)[None, :]
    ).astype(BF16)
    same = own_unit[:, None] // head == grad_unit[None, :] // head
    spread_back = jnp.where(same, dot(gate_own, chosen, 1, 0), 0.0).astype(BF16)
    conv_grad = direct + dot(grad_pair, spread_back, 0, 1)
    halo = shift(conv_grad.reshape(dp_count, stretch, units)[:, :8], -1).reshape(-1, units)
    x_grad, conv_sums = run(
        functools.partial(conv_back_kernel, parts), order, (conv_grad, x_rel, halo, masks, params),
        (shape(BF16), sums), buffer,
    )
    in_grad = scatter_plane(
        dot(x_grad[:mid], w_x, 1, 0) + dot(y_grad[:mid], w_y, 1, 0),
        (dot(x_grad[mid:], w_x, 1, 0) + dot(y_grad[mid:], w_y, 1, 0)).astype(BF16),
    )
    in_grad, mlp_grad = lax.optimization_barrier((in_grad, mlp_grad))
    _, first_pull = jax.vjp(rms_norm, resid_in, gain_one)
    stream_norm_grad, gain_one_grad = first_pull(in_grad)
    stream_grad = resid_grad + stream_norm_grad
    late = after(tuple(hidden), all_resid)
    out_stream = resid_mid + scatter_line([dot(step(late, k), w_d, 1, 0) for k in range(chips)])

    grads_o = scatter_chips(dot(mixed, all_resid, 0, 0).astype(BF16))
    grads_y = scatter_chips(dot(y_grad, all_in, 0, 0).astype(BF16))
    grads_x = scatter_chips(dot(x_grad, all_in, 0, 0).astype(BF16))
    rec_grad = jnp.stack([grads_x, grads_y, grads_o], axis=1)
    dense = jnp.where(same, dot(conv_rows, grad_pair, 1, 1), 0.0).astype(BF16)
    gate_term = dot(dense, chosen, 1, 1)
    unit_sums = jnp.concatenate([conv_sums[:5], gate_sums[:3], jnp.zeros((120, units), F32)], axis=0).T
    unit_shard = scatter_chips(jnp.concatenate([gate_term, unit_sums], axis=1))
    gate_shard = unit_shard[:, : 2 * head].reshape(shard, 2, head)
    unit_shard = unit_shard[:, 2 * head : 2 * head + 8].T

    gains_term = jnp.stack([gain_one_grad, gain_two_grad]).reshape(2, dp_count, seq_count, shard)
    gains_shard = small_sum_dp(small_sum_seq(jnp.transpose(gains_term, (2, 1, 0, 3))))
    return (
        out_stream[None],
        stream_grad[None],
        rec_grad,
        gate_shard,
        mlp_grad,
        gains_shard,
        unit_shard[0:4],
        unit_shard[4:7],
        unit_shard[7],
    )


def solution(mesh):
    placed = (
        P("dp", "seq", None),
        P("dp", "seq"),
        P(("dp", "seq"), None, None),
        P(("dp", "seq"), None, None),
        P(("dp", "seq"), None, None),
        P(None, ("dp", "seq")),
        P(None, ("dp", "seq")),
        P(None, ("dp", "seq")),
        P(("dp", "seq")),
        P("dp", "seq", None),
    )
    return jax.shard_map(
        per_device,
        mesh=mesh,
        in_specs=placed,
        out_specs=(
            P("dp", "seq", None),
            P("dp", "seq", None),
            P(("dp", "seq"), None, None),
            P(("dp", "seq"), None, None),
            P(("dp", "seq"), None, None),
            P(None, ("dp", "seq")),
            P(None, ("dp", "seq")),
            P(None, ("dp", "seq")),
            P(("dp", "seq")),
        ),
        check_vma=False,
    )
```

```python
import functools

import jax
import jax.numpy as jnp
from jax import lax
from jax.experimental import pallas as pl
from jax.experimental.pallas import tpu as pltpu
from jax.sharding import PartitionSpec as P


EPS = 1e-06
GELU_ROOT = 0.7978845608028654
GELU_CUBE = 0.044715
F32 = jnp.float32
BF16 = jnp.bfloat16


def gelu_tanh(values):
    inner_arg = GELU_ROOT * (values + GELU_CUBE * values * values * values)
    return 0.5 * values * (1.0 + jnp.tanh(inner_arg))


def gelu_both(values):
    inner_arg = GELU_ROOT * (values + GELU_CUBE * values * values * values)
    tanh_value = jnp.tanh(inner_arg)
    half_sum = 0.5 * (1.0 + tanh_value)
    slope = half_sum + 0.5 * values * (1.0 - tanh_value * tanh_value) * GELU_ROOT * (
        1.0 + 3.0 * GELU_CUBE * values * values
    )
    return values * half_sum, slope


def rms_norm(stream, gain_vec):
    scaling = lax.rsqrt(jnp.mean(stream * stream, axis=-1, keepdims=True) + EPS)
    return stream * scaling * gain_vec


def dot(left, right, left_dim, right_dim):
    return lax.dot_general(
        left, right, (((left_dim,), (right_dim,)), ((), ())), preferred_element_type=F32
    )


def join_kernel(*refs):
    pieces, out_ref, sems = refs[:-2], refs[-2], refs[-1]
    copies, start = [], 0
    for n, piece in enumerate(pieces):
        rows = piece.shape[0]
        copies.append(pltpu.make_async_copy(piece, out_ref.at[pl.ds(start, rows)], sems.at[n]))
        start += rows
    for copy in copies:
        copy.start()
    for copy in copies:
        copy.wait()


def join(pieces):
    rows, width = sum(a.shape[0] for a in pieces), pieces[0].shape[1]
    size = rows * width * 2
    return pl.pallas_call(
        join_kernel,
        in_specs=[pl.BlockSpec(memory_space=pl.ANY)] * len(pieces),
        out_specs=pl.BlockSpec(memory_space=pltpu.VMEM),
        out_shape=jax.ShapeDtypeStruct((rows, width), pieces[0].dtype),
        scratch_shapes=[pltpu.SemaphoreType.DMA((len(pieces),))],
        compiler_params=pltpu.CompilerParams(vmem_limit_bytes=56 << 20),
        cost_estimate=pl.CostEstimate(flops=0, bytes_accessed=2 * size, transcendentals=0),
    )(*pieces)


def after(value, *others):
    return lax.optimization_barrier((value,) + others)[0]


def blocks_kernel(order, x_ref, out_ref, sem):
    count = order.shape[0]
    rows = x_ref.shape[0] // count
    copies = [
        pltpu.make_async_copy(x_ref.at[rows_of(order[i], rows)], out_ref.at[pl.ds(i * rows, rows)], sem.at[i])
        for i in range(count)
    ]
    for copy in copies:
        copy.start()
    for copy in copies:
        copy.wait()


def take_blocks(order, value):
    size = value.size * 4
    return pl.pallas_call(
        blocks_kernel,
        in_specs=[pl.BlockSpec(memory_space=pltpu.SMEM), pl.BlockSpec(memory_space=pl.ANY)],
        out_specs=pl.BlockSpec(memory_space=pltpu.VMEM),
        out_shape=jax.ShapeDtypeStruct(value.shape, value.dtype),
        scratch_shapes=[pltpu.SemaphoreType.DMA((order.shape[0],))],
        compiler_params=pltpu.CompilerParams(vmem_limit_bytes=56 << 20),
        cost_estimate=pl.CostEstimate(flops=0, bytes_accessed=size, transcendentals=0),
    )(order, value)


def swap(value):
    count = lax.axis_size("seq")
    return lax.ppermute(value, "seq", [(i, i ^ 1) for i in range(count)])


def shift(value, step):
    count = lax.axis_size("seq")
    return lax.ppermute(value, "seq", [(i, (i + 2 * step) % count) for i in range(count)])


def cross(value, bit):
    count = lax.axis_size("dp")
    return lax.ppermute(value, "dp", [(i, i ^ bit) for i in range(count)])


def rows_at(value, chip, offset, size, own):
    chips = lax.axis_size("seq") // 2
    return lax.dynamic_slice(value, ((chip % chips) * own + offset, 0), (size, value.shape[1]))


def core_groups():
    count = lax.axis_size("seq")
    return [list(range(core, count, 2)) for core in range(2)]


def gather_chips(own, gates=()):
    chips, chip = lax.axis_size("seq") // 2, lax.axis_index("seq") // 2
    rows = own.shape[0]
    half = rows // 2
    up, down = own[:half], own[half:]
    whole = jnp.zeros((chips * rows, own.shape[1]), own.dtype)
    whole = lax.dynamic_update_slice(whole, own, (chip * rows, 0))
    for k in range(1, chips):
        if k < len(gates) and gates[k] is not None:
            up, down = after((up, down), gates[k])
        up, down = shift(up, 1), shift(down, -1)
        whole = lax.dynamic_update_slice(whole, up, (((chip - k) % chips) * rows, 0))
        whole = lax.dynamic_update_slice(whole, down, (((chip + k) % chips) * rows + half, 0))
    return whole


def scatter_chips(terms, gates=()):
    chips, chip = lax.axis_size("seq") // 2, lax.axis_index("seq") // 2
    own = terms.shape[0] // chips
    half = own // 2

    def level(k):
        up, down = rows_at(terms, chip - k, 0, half, own), rows_at(terms, chip + k, half, half, own)
        return up.astype(F32), down.astype(F32)

    up, down = level(1 % chips)
    for j in range(1, chips):
        next_up, next_down = level((j + 1) % chips)
        up, down = up.astype(BF16), down.astype(BF16)
        if j < len(gates):
            up, down = after((up, down), gates[j])
        up = next_up + shift(up, 1).astype(F32)
        down = next_down + shift(down, -1).astype(F32)
    return jnp.concatenate([up, down], axis=0)


def gather_line(own, gates=()):
    half = own.shape[0] // 2
    up, down = own[:half], own[half:]
    near = []
    for k in range(1, lax.axis_size("seq") // 2):
        if k < len(gates) and gates[k] is not None:
            up, down = after((up, down), gates[k])
        up, down = shift(up, 1), shift(down, -1)
        near += [up, down]
    near.append(own)
    return join(near + [swap(a) for a in near])


def scatter_line(mine, other, work=()):
    chips = lax.axis_size("seq") // 2
    block = mine.shape[0] // chips
    half = block // 2
    sent = [swap(other[:block])] + ([swap(other[block:])] if chips > 1 else [])

    def level(j):
        theirs = sent[0] if j == 0 else sent[1][(j - 1) * block : j * block]
        terms = mine[j * block : (j + 1) * block] + theirs.astype(F32)
        return terms[:half], terms[half:]

    up, down = level(0)
    results = []
    for j in range(1, chips):
        next_up, next_down = level(j)
        up, down = up.astype(BF16), down.astype(BF16)
        if j <= len(work):
            results.append(work[j - 1]((up, down)))
        up = shift(up, 1)
        down = shift(down, -1)
        if j <= len(work):
            up, down = after((up, down), results[-1])
        up, down = next_up + up.astype(F32), next_down + down.astype(F32)
    return jnp.concatenate([up, down], axis=0), results


def gather_plane(own):
    half = own.shape[0] // 2
    first, second = cross(own, 1), cross(own, 2)
    third = [cross(first[:half], 2), cross(second[half:], 1)]
    near = [own, first, second] + third
    return join(near + [swap(a) for a in near])


def scatter_plane(mine, other, gate=None):
    block = mine.shape[0] // 4
    half = block // 2
    far = mine[3 * block :] + swap(other[3 * block :]).astype(F32)
    far = far.astype(BF16)
    near = mine[: 3 * block] + swap(other[: 3 * block]).astype(F32)
    here, first, second = near[:block], near[block : 2 * block], near[2 * block :]
    top, low = cross(far[:half], 2).astype(F32), cross(far[half:], 1).astype(F32)
    first = jnp.concatenate([first[:half] + top, first[half:]], axis=0).astype(BF16)
    second = jnp.concatenate([second[:half], second[half:] + low], axis=0).astype(BF16)
    if gate is not None:
        first, second = after((first, second), gate)
    return here + cross(first, 1).astype(F32) + cross(second, 2).astype(F32)


def gather_pair(own):
    first = cross(own, 1)
    return join([own, swap(own), first, swap(first)])


def small_gather(value):
    dp_count, seq_count = lax.axis_size("dp"), lax.axis_size("seq")
    dp_place, seq_place = lax.axis_index("dp"), lax.axis_index("seq")
    near = jnp.stack([value] + [cross(value, e) for e in range(1, dp_count)])
    rounds = [(lambda i, k=k: (i + k) % seq_count) for k in range(seq_count)]
    every = [near] + [
        lax.ppermute(near, "seq", [(i, to(i)) for i in range(seq_count)]) for to in rounds[1:]
    ]
    every = jnp.stack(every).reshape(seq_count * dp_count, -1)
    spot = jnp.arange(seq_count * dp_count)
    source = ((seq_place - spot // dp_count) % seq_count) * dp_count + ((spot % dp_count) ^ dp_place)
    return dot((source[:, None] == spot[None, :]).astype(BF16), every, 1, 0).astype(BF16)


def small_sum_seq(terms):
    count = lax.axis_size("seq")
    place = lax.axis_index("seq")
    total = lax.dynamic_index_in_dim(terms, place, 0, False)
    for k in range(1, count):
        sent = lax.dynamic_index_in_dim(terms, (place + k) % count, 0, False)
        total = total + lax.ppermute(sent, "seq", [(i, (i + k) % count) for i in range(count)])
    return total


def small_sum_dp(terms):
    count = lax.axis_size("dp")
    place = lax.axis_index("dp")
    total = lax.dynamic_index_in_dim(terms, place, 0, False)
    for k in range(1, count):
        sent = lax.dynamic_index_in_dim(terms, (place + k) % count, 0, False)
        total = total + lax.ppermute(sent, "dp", [(i, (i + k) % count) for i in range(count)])
    return total


def rows_of(index, size):
    return pl.ds(pl.multiple_of(index * size, size), size)


def conv_kernel(parts, order, x_ref, halo_ref, mask_ref, prm_ref, out_ref, buf):
    rows = buf.shape[0] - 8

    def one(i, carry):
        @pl.when(i % parts == 0)
        def _():
            buf[0:8, :] = halo_ref[rows_of(i // parts, 8), :]

        x = x_ref[rows_of(order[i], rows), :].astype(F32)
        buf[8 : 8 + rows, :] = x
        mask = mask_ref[rows_of(i, rows), :]
        total = prm_ref[4:5, :] + jnp.where(mask[:, 0:1] > 0.0, prm_ref[0:1, :] * x, 0.0)
        for k in range(1, 4):
            late = buf[8 - k : 8 - k + rows, :]
            total = total + jnp.where(mask[:, k : k + 1] > 0.0, prm_ref[k : k + 1, :] * late, 0.0)
        out_ref[rows_of(i, rows), :] = total.astype(BF16)
        buf[0:8, :] = x[rows - 8 :, :]
        return carry

    lax.fori_loop(0, x_ref.shape[0] // rows, one, 0)


def minus_expm1(v):
    series = v * (1.0 / 10.0)
    for n in range(9, 1, -1):
        series = (1.0 + series) * v * (1.0 / n)
    return jnp.where(v > -0.5, -v * (1.0 + series), 1.0 - jnp.exp(v))


def gates(rate, admit, prm_ref, start):
    recur_gate = jax.nn.sigmoid(rate + prm_ref[5:6, :])
    admit_gate = jax.nn.sigmoid(admit + prm_ref[6:7, :])
    log_decay = -8.0 * prm_ref[8:9, :] * (0.5 + 0.5 * recur_gate)
    decay = jnp.where(start, 0.0, jnp.exp(log_decay))
    scale = jnp.where(start, 1.0, jnp.sqrt(minus_expm1(2.0 * log_decay)))
    return recur_gate, admit_gate, decay, scale


def scan_rows(mult, add, carry, reverse):
    rows = mult.shape[0]
    place = lax.broadcasted_iota(jnp.int32, mult.shape, 0) % 8
    for step in (1, 2, 4):
        turn = rows - step if reverse else step
        inside = (place < 8 - step) if reverse else (place >= step)
        prev_mult = jnp.where(inside, pltpu.roll(mult, turn, 0), 1.0)
        prev_add = jnp.where(inside, pltpu.roll(add, turn, 0), 0.0)
        add = mult * prev_add + add
        mult = mult * prev_mult
    sums, products = [], []
    order = range(rows // 8)
    for tile in reversed(order) if reverse else order:
        lead = mult[tile * 8 : tile * 8 + 8]
        part = add[tile * 8 : tile * 8 + 8] + lead * carry[0]
        lead = lead * carry[1]
        carry = (part[0:1], lead[0:1]) if reverse else (part[7:8], lead[7:8])
        sums.append(part)
        products.append(lead)
    if reverse:
        sums, products = sums[::-1], products[::-1]
    return jnp.concatenate(sums, axis=0), jnp.concatenate(products, axis=0), carry


def fresh(begin, carry):
    return jnp.where(begin, 0.0, carry[0]), jnp.where(begin, 1.0, carry[1])


def blank(width):
    return jnp.zeros((1, width), F32), jnp.ones((1, width), F32)


def local_kernel(rows, parts, rate_ref, admit_ref, conv_ref, mask_ref, prm_ref, local_ref, lead_ref, decay_ref, recur_ref, enter_ref, scale_ref, ends_ref):
    count = rate_ref.shape[0] // rows

    def one(i, carry):
        here = rows_of(i, rows)
        start = mask_ref[here, :][:, 1:2] < 0.5
        recur_gate, admit_gate, decay, scale = gates(rate_ref[here, :], admit_ref[here, :], prm_ref, start)
        recur_ref[here, :] = recur_gate
        enter_ref[here, :] = admit_gate
        scale_ref[here, :] = scale
        drive = scale * admit_gate * conv_ref[here, :].astype(F32)
        local, lead, carry = scan_rows(decay, drive, fresh(i % parts == 0, carry), False)
        local_ref[here, :] = local
        lead_ref[here, :] = lead
        decay_ref[here, :] = decay
        ends_ref[pl.ds(i // parts, 1), :] = carry[0]
        ends_ref[pl.ds(count // parts + i // parts, 1), :] = carry[1]
        return carry

    lax.fori_loop(0, count, one, blank(rate_ref.shape[1]))


def state_kernel(rows, parts, order, local_ref, lead_ref, y_ref, enter_ref, state_ref, prev_ref, mixed_ref):
    def one(i, carry):
        here, there = rows_of(i, rows), rows_of(order[i], rows)
        enter = enter_ref[pl.ds(i // parts, 1), :]
        carry = jnp.where(i % parts == 0, enter, carry)
        state = local_ref[here, :] + lead_ref[here, :] * enter
        top = lax.broadcasted_iota(jnp.int32, state.shape, 0) == 0
        state_ref[here, :] = state
        prev_ref[here, :] = jnp.where(top, carry, pltpu.roll(state, 1, 0))
        mixed_ref[there, :] = (state * gelu_tanh(y_ref[there, :])).astype(BF16)
        return state[rows - 1 :, :]

    lax.fori_loop(0, local_ref.shape[0] // rows, one, jnp.zeros((1, local_ref.shape[1]), F32))


def flow_kernel(rows, parts, order, grad_ref, y_ref, decay_ref, flow_ref, lead_ref, state_grad_ref, ends_ref):
    count = grad_ref.shape[0] // rows

    def one(lap, carry):
        i = count - 1 - lap
        here, there = rows_of(i, rows), rows_of(order[i], rows)
        state_grad = grad_ref[there, :] * gelu_tanh(y_ref[there, :])
        decay = decay_ref[here, :]
        carry = fresh(i % parts == parts - 1, carry)
        flow, lead, carry = scan_rows(decay, decay * state_grad, carry, True)
        flow_ref[here, :] = flow
        lead_ref[here, :] = lead
        state_grad_ref[here, :] = state_grad
        ends_ref[pl.ds(i // parts, 1), :] = carry[0]
        ends_ref[pl.ds(count // parts + i // parts, 1), :] = carry[1]
        return carry

    lax.fori_loop(0, count, one, blank(grad_ref.shape[1]))


def adjoint_kernel(
    rows, parts, order, flow_ref, lead_ref, state_grad_ref, enter_ref, grad_ref, y_ref, state_ref, prev_ref,
    decay_ref, recur_ref, admit_ref, scale_ref, conv_ref, mask_ref, prm_ref, y_grad_ref, rate_grad_ref, admit_grad_ref, direct_ref, sums_ref,
):
    count = decay_ref.shape[0] // rows
    sums_ref[...] = jnp.zeros_like(sums_ref)

    def one(lap, carry):
        i = count - 1 - lap
        here, there = rows_of(i, rows), rows_of(order[i], rows)
        start = mask_ref[here, :][:, 1:2] < 0.5
        recur_gate, admit_gate = recur_ref[here, :], admit_ref[here, :]
        decay, scale = decay_ref[here, :], scale_ref[here, :]
        conv = conv_ref[here, :].astype(F32)
        _, y_slope = gelu_both(y_ref[there, :])
        y_grad_ref[there, :] = (grad_ref[there, :] * state_ref[here, :] * y_slope).astype(BF16)
        enter = enter_ref[pl.ds(i // parts, 1), :]
        carry = jnp.where(i % parts == parts - 1, enter, carry)
        flow = flow_ref[here, :] + lead_ref[here, :] * enter
        last = lax.broadcasted_iota(jnp.int32, flow.shape, 0) == rows - 1
        adjoint = state_grad_ref[here, :] + jnp.where(last, carry, pltpu.roll(flow, rows - 1, 0))
        scaled = adjoint * scale
        scale_grad = adjoint * admit_gate * conv
        log_grad = jnp.where(
            start, 0.0, adjoint * prev_ref[here, :] * decay - scale_grad * (decay * decay) / scale
        )
        rate_grad = log_grad * (-4.0 * prm_ref[8:9, :]) * (recur_gate * (1.0 - recur_gate))
        admit_grad = scaled * conv * (admit_gate * (1.0 - admit_gate))
        direct_ref[here, :] = scaled * admit_gate
        rate_grad_ref[here, :] = rate_grad.astype(BF16)
        admit_grad_ref[here, :] = admit_grad.astype(BF16)
        sums_ref[0:1, :] += jnp.sum(rate_grad, axis=0, keepdims=True)
        sums_ref[1:2, :] += jnp.sum(admit_grad, axis=0, keepdims=True)
        sums_ref[2:3, :] += jnp.sum(log_grad * (-4.0 - 4.0 * recur_gate), axis=0, keepdims=True)
        return flow[0:1, :]

    lax.fori_loop(0, count, one, jnp.zeros((1, decay_ref.shape[1]), F32))
    sums_ref[2:3, :] = sums_ref[2:3, :] * prm_ref[9:10, :]


def conv_back_kernel(parts, order, grad_ref, x_ref, halo_ref, mask_ref, prm_ref, x_grad_ref, sums_ref, buf):
    rows = buf.shape[0] - 8
    count = grad_ref.shape[0] // rows
    sums_ref[...] = jnp.zeros_like(sums_ref)

    def one(lap, carry):
        i = count - 1 - lap
        here, there = rows_of(i, rows), rows_of(order[i], rows)

        @pl.when(i % parts == parts - 1)
        def _():
            buf[rows : rows + 8, :] = halo_ref[rows_of(i // parts, 8), :]

        grad = grad_ref[here, :]
        buf[0:rows, :] = grad
        x = x_ref[there, :].astype(F32)
        mask = mask_ref[here, :]
        total = jnp.zeros_like(grad)
        for k in range(4):
            late = jnp.where(mask[:, 4 + k : 5 + k] > 0.0, buf[k : k + rows, :], 0.0)
            total = total + prm_ref[k : k + 1, :] * late
            sums_ref[k : k + 1, :] += jnp.sum(late * x, axis=0, keepdims=True)
        sums_ref[4:5, :] += jnp.sum(grad, axis=0, keepdims=True)
        x_grad_ref[there, :] = total.astype(BF16)
        buf[rows : rows + 8, :] = grad[0:8, :]
        return carry

    lax.fori_loop(0, count, one, 0)


def run(kernel, order, inputs, outs, scratch=()):
    whole = pl.BlockSpec(memory_space=pltpu.VMEM)
    table = () if order is None else (order,)
    size = sum(a.size * 4 for a in inputs) + sum(4 * s.size for s in outs)
    return pl.pallas_call(
        kernel,
        in_specs=[pl.BlockSpec(memory_space=pltpu.SMEM)] * len(table) + [whole] * len(inputs),
        out_specs=[whole] * len(outs),
        out_shape=list(outs),
        scratch_shapes=list(scratch),
        compiler_params=pltpu.CompilerParams(vmem_limit_bytes=56 << 20),
        cost_estimate=pl.CostEstimate(flops=50 * size, bytes_accessed=size, transcendentals=size),
    )(*table, *inputs)


def enter_from(ends, reverse):
    chips = lax.axis_size("seq") // 2
    chip = lax.axis_index("seq") // 2
    count = ends.shape[0] // 2
    state = jnp.zeros((count, ends.shape[1]), F32)
    for k in range(chips - 1, 0, -1):
        sent = shift(ends, -k if reverse else k)
        there = (chip + k < chips) if reverse else (chip >= k)
        state = jnp.where(there, sent[:count] + sent[count:] * state, state)
    return state


def per_device(
    stream, seg_ids, rec_weight, gate_weight, mlp_weight, norm_gains, conv_weight, lru_biases, decay_param, cotangent
):
    resid_in, doc_ids, out_grad = stream[0], seg_ids[0], cotangent[0]
    block, width = resid_in.shape
    dp_count, seq_count = lax.axis_size("dp"), lax.axis_size("seq")
    dp_place, seq_place = lax.axis_index("dp"), lax.axis_index("seq")
    chip_place, core_place = seq_place // 2, seq_place % 2
    chips = seq_count // 2
    half = block // 2
    stretch = 2 * block
    tokens = dp_count * stretch
    parts = stretch // half
    shard, head = rec_weight.shape[0], gate_weight.shape[2]
    units = shard * chips

    place = jnp.arange(dp_count * parts)
    order = (
        (((place // 2) % 2) ^ core_place) * dp_count + ((place // parts) ^ dp_place)
    ) * 2 + place % 2
    order = order.astype(jnp.int32)

    def unit_id(dp_index, core_index, row):
        return (dp_index * seq_count + (row // shard) * 2 + core_index) * shard + row % shard

    own_unit = unit_id(dp_place, core_place, jnp.arange(units))
    spot = jnp.arange(4 * units)
    pair_unit = unit_id(dp_place ^ (spot // (2 * units)), core_place ^ ((spot // units) % 2), spot % units)
    spot = jnp.arange(8 * units)
    grad_unit = unit_id(
        dp_place ^ (spot // (4 * units)), core_place ^ ((spot // (2 * units)) % 2), spot % units
    )
    grad_kind = (spot // units) % 2

    small = jnp.concatenate([norm_gains, conv_weight, lru_biases, decay_param[None]], axis=0)
    small = jnp.concatenate([small.reshape(-1), doc_ids.astype(BF16)])
    length = small.shape[0]
    small = jnp.pad(small, (0, -length % 128)).reshape(-1, 128)
    small = small_gather(small).reshape(seq_count, dp_count, -1)
    ids = jnp.transpose(small[:, :, 10 * shard : length], (1, 0, 2)).reshape(dp_count, -1).astype(jnp.int32)
    small = small[:, :, : 10 * shard].reshape(seq_count, dp_count, 10, shard)
    small = jnp.transpose(small, (2, 1, 0, 3)).reshape(10, width)
    gain_one, gain_two = small[0].astype(F32), small[1].astype(F32)

    first = jnp.concatenate([rec_weight[:, 0, :], gate_weight.reshape(shard, 2 * head)], axis=1)
    first = lax.all_gather(first, "seq", axis=0, tiled=True, axis_index_groups=core_groups())
    w_x, gate_own = first[:, :width], first[:, width:]
    mlp_rows = jnp.concatenate([mlp_weight[:, n, :] for n in range(3)], axis=1)
    mlp_full = lax.all_gather(after(mlp_rows, gain_one), "dp", axis=0, tiled=True)
    w_g, w_u, w_d = (mlp_full[:, n * width : (n + 1) * width] for n in range(3))

    own = (jnp.arange(width)[:, None] == own_unit[None, :]).astype(BF16)
    own = dot(small[2:], own, 1, 0)
    decay_raw = own[7]
    params = jnp.concatenate(
        [own, jax.nn.softplus(decay_raw)[None], jax.nn.sigmoid(decay_raw)[None], jnp.zeros((6, units), F32)]
    )
    near_ids = lax.dynamic_slice(
        jnp.pad(ids, ((0, 0), (3, 3)), constant_values=-1), (0, chip_place * stretch), (dp_count, stretch + 6)
    )
    masks = [near_ids[:, 3 : 3 + stretch] == near_ids[:, 3 - k : 3 - k + stretch] for k in range(4)]
    masks += [near_ids[:, 3 : 3 + stretch] == near_ids[:, 3 + k : 3 + k + stretch] for k in range(4)]
    masks = jnp.stack(masks, axis=-1).astype(F32).reshape(tokens, 8)

    normed_in = rms_norm(resid_in, gain_one).astype(BF16)
    all_in = gather_plane(normed_in)
    later = rec_weight[:, 1:, :].reshape(shard, 2 * width)
    later = gather_chips(later, (gain_one, gain_one, gain_one, all_in))
    w_y, w_o = later[:, :width], later[:, width:]
    x_rel = dot(all_in, w_x, 1, 1).astype(BF16)
    shape = lambda dtype: jax.ShapeDtypeStruct((tokens, units), dtype)
    totals = jax.ShapeDtypeStruct((8, units), F32)
    ends = jax.ShapeDtypeStruct((2 * dp_count, units), F32)
    buffer = (pltpu.VMEM((half + 8, units), F32),)
    call = lambda kernel: functools.partial(kernel, half, parts)
    tails = x_rel.reshape(-1, half, units)[:, half - 8 :]
    tails = jnp.take(tails, order[parts - 1 :: parts], axis=0)
    halo = shift(tails, 1).astype(F32).reshape(-1, units)
    (conv_out,) = run(
        functools.partial(conv_kernel, parts), order, (x_rel, halo, masks, params), (shape(BF16),), buffer
    )
    conv_rows = conv_out.T

    gate_pair = gather_pair(gate_own)
    own_column = jnp.concatenate([own_unit % head, own_unit % head + head])
    pick = (jnp.arange(2 * head)[:, None] == own_column[None, :]).astype(BF16)
    own_heads = jnp.concatenate([own_unit // head] * 2)
    spread = jnp.where(
        pair_unit[:, None] // head == own_heads[None, :], dot(gate_pair, pick, 1, 0), 0.0
    ).astype(BF16)
    y_rel = dot(all_in, w_y, 1, 1)
    conv_pair = after(gather_pair(conv_rows), y_rel)
    rate_pre = dot(conv_pair, spread[:, :units], 0, 0)
    admit_pre = dot(conv_pair, spread[:, units:], 0, 0)
    local, lead, decay, recur_gate, admit_gate, scale, tops = run(
        call(local_kernel), None, (rate_pre, admit_pre, conv_out, masks, params), (shape(F32),) * 6 + (ends,)
    )
    state, state_prev, mixed = run(
        call(state_kernel), order, (local, lead, y_rel, enter_from(tops, False)),
        (shape(F32), shape(F32), shape(BF16)),
    )
    mid = tokens // 2
    all_grad = gather_line(out_grad.astype(BF16), (conv_out, conv_out, conv_pair, tops))
    resid_mid = resid_in + scatter_plane(
        dot(mixed[:mid], w_o, 1, 0), dot(mixed[mid:], w_o, 1, 0).astype(BF16), all_grad
    )

    normed_mid = rms_norm(resid_mid, gain_two).astype(BF16)
    hidden_grad = dot(all_grad, w_d, 1, 1)
    all_mid = gather_line(normed_mid, (None, None, None, hidden_grad))
    gate_pre, up_pre = dot(all_mid, w_g, 1, 1), dot(all_mid, w_u, 1, 1)
    act, slope = gelu_both(gate_pre)
    hidden = (act * up_pre).astype(BF16)
    gate_grad = (hidden_grad * up_pre * slope).astype(BF16)
    up_grad = (hidden_grad * act).astype(BF16)
    line = all_mid.shape[0] // 2
    mid_mine, mid_other = (
        dot(a, w_g, 1, 0) + dot(b, w_u, 1, 0)
        for a, b in ((gate_grad[:line], up_grad[:line]), (gate_grad[line:], up_grad[line:]))
    )
    weight_work = [
        lambda ready, a=a, b=b: dot(after(a, *ready), b, 0, 0).astype(BF16)
        for a, b in ((gate_grad, all_mid), (up_grad, all_mid), (hidden, all_grad))
    ]
    mid_grad, sums = scatter_line(mid_mine, mid_other.astype(BF16), weight_work)
    mlp_sums = [lax.psum_scatter(a, "dp", scatter_dimension=0, tiled=True) for a in sums]
    mlp_grad = jnp.stack(mlp_sums, axis=1)

    _, norm_pull = jax.vjp(rms_norm, resid_mid, gain_two)
    resid_norm_grad, gain_two_grad = norm_pull(mid_grad)
    resid_grad = out_grad + resid_norm_grad
    all_resid = gather_plane(resid_grad.astype(BF16))
    mixed_grad = dot(all_resid, w_o, 1, 1)
    flow, flow_lead, state_grad, heads_up = run(
        call(flow_kernel), order, (mixed_grad, y_rel, decay), (shape(F32), shape(F32), shape(F32), ends)
    )
    y_grad, rate_grad, admit_grad, direct, gate_sums = run(
        call(adjoint_kernel), order,
        (
            flow, flow_lead, state_grad, enter_from(heads_up, True), mixed_grad, y_rel, state, state_prev,
            decay, recur_gate, admit_gate, scale, conv_out, masks, params,
        ),
        (shape(BF16), shape(BF16), shape(BF16), shape(F32), totals),
    )
    grad_pair = gather_pair(jnp.concatenate([rate_grad.T, admit_grad.T], axis=0))
    chosen = (
        jnp.arange(2 * head)[:, None] == (grad_unit % head + grad_kind * head)[None, :]
    ).astype(BF16)
    same = own_unit[:, None] // head == grad_unit[None, :] // head
    spread_back = jnp.where(same, dot(gate_own, chosen, 1, 0), 0.0).astype(BF16)
    conv_grad = direct + dot(grad_pair, spread_back, 0, 1)
    halo = shift(conv_grad.reshape(dp_count, stretch, units)[:, :8], -1).reshape(-1, units)
    x_grad, conv_sums = run(
        functools.partial(conv_back_kernel, parts), order, (conv_grad, x_rel, halo, masks, params),
        (shape(BF16), totals), buffer,
    )
    in_other = (dot(x_grad[mid:], w_x, 1, 0) + dot(y_grad[mid:], w_y, 1, 0)).astype(BF16)
    in_grad = scatter_plane(dot(x_grad[:mid], w_x, 1, 0) + dot(y_grad[:mid], w_y, 1, 0), in_other)
    _, first_pull = jax.vjp(rms_norm, resid_in, gain_one)
    stream_norm_grad, gain_one_grad = first_pull(in_grad)
    stream_grad = resid_grad + stream_norm_grad
    spot = jnp.arange(2 * seq_count)
    away = jnp.where(spot % 2 == 0, chip_place - spot // 4, spot // 4 - chip_place) % chips
    line_order = (((spot // 2) % 2) ^ core_place) * 2 * chips + ((away - 1) % chips) * 2 + spot % 2
    late = take_blocks(line_order.astype(jnp.int32), after(hidden, grad_pair, *mlp_sums))
    out_sum = lax.psum_scatter(dot(late, w_d, 1, 0).astype(BF16), "seq", scatter_dimension=0, tiled=True)
    out_stream = resid_mid + out_sum.astype(F32)

    grads_oy = jnp.concatenate([dot(mixed, all_resid, 0, 0), dot(y_grad, all_in, 0, 0)], axis=1).astype(BF16)
    grads_oy = lax.psum_scatter(
        after(grads_oy, x_grad, *mlp_sums), "seq", scatter_dimension=0, tiled=True, axis_index_groups=core_groups()
    ).astype(F32)
    grads_x = scatter_chips(dot(after(x_grad, in_other), all_in, 0, 0).astype(BF16))
    rec_grad = jnp.stack([grads_x, grads_oy[:, width:], grads_oy[:, :width]], axis=1)
    dense = jnp.where(same, dot(conv_rows, grad_pair, 1, 1), 0.0).astype(BF16)
    gate_term = dot(dense, chosen, 1, 1)
    unit_sums = jnp.concatenate([conv_sums[:5], gate_sums[:3], jnp.zeros((120, units), F32)], axis=0).T
    unit_shard = scatter_chips(jnp.concatenate([gate_term, unit_sums], axis=1))
    gate_shard = unit_shard[:, : 2 * head].reshape(shard, 2, head)
    unit_shard = unit_shard[:, 2 * head : 2 * head + 8].T

    gains_term = jnp.stack([gain_one_grad, gain_two_grad]).reshape(2, dp_count, seq_count, shard)
    gains_term = jnp.transpose(gains_term, (2, 1, 0, 3))
    mlp_grad = after(mlp_grad, gains_term).astype(F32)
    gains_shard = small_sum_dp(after(small_sum_seq(gains_term), mlp_grad))
    return (
        out_stream[None],
        stream_grad[None],
        rec_grad,
        gate_shard,
        mlp_grad,
        gains_shard,
        unit_shard[0:4],
        unit_shard[4:7],
        unit_shard[7],
    )


def solution(mesh):
    placed = (
        P("dp", "seq", None),
        P("dp", "seq"),
        P(("dp", "seq"), None, None),
        P(("dp", "seq"), None, None),
        P(("dp", "seq"), None, None),
        P(None, ("dp", "seq")),
        P(None, ("dp", "seq")),
        P(None, ("dp", "seq")),
        P(("dp", "seq")),
        P("dp", "seq", None),
    )

    return jax.shard_map(
        per_device,
        mesh=mesh,
        in_specs=placed,
        out_specs=(
            P("dp", "seq", None),
            P("dp", "seq", None),
            P(("dp", "seq"), None, None),
            P(("dp", "seq"), None, None),
            P(("dp", "seq"), None, None),
            P(None, ("dp", "seq")),
            P(None, ("dp", "seq")),
            P(None, ("dp", "seq")),
            P(("dp", "seq")),
        ),
        check_vma=False,
    )
```
